32 devices in a mesh: replica: 8 (over z, core), tensor: 4 (over y, x).
Axes of the slice: x: 2, y: 2, z: 4, core: 2. Of those that a mesh axis runs over, the one named last changes fastest.
Arguments:
- hidden: bfloat16 [3, 64, 8192], P(None, None, 'replica'), may hold values from -6 to 6
- parents: int32 [3, 64], replicated, may hold values from 0 to 63, as said below
- input_weight: bfloat16 [8192, 2, 8192], P('replica', None, 'tensor'), may hold values from -0.0625 to 0.0625
- coeff_weight: bfloat16 [8192, 2, 512], P('replica'), may hold values from -0.0625 to 0.0625
- step_weight: bfloat16 [8192, 128], P('replica', 'tensor'), may hold values from -0.0625 to 0.0625
- kernel_x: float32 [4, 8192], P(None, 'tensor'), may hold values from -0.5 to 0.5
- kernel_bias_x: float32 [8192], P('tensor'), may hold values from -0.5 to 0.5
- kernel_coeff: float32 [4, 2, 512], replicated, may hold values from -0.5 to 0.5
- kernel_bias_coeff: float32 [2, 512], replicated, may hold values from -0.5 to 0.5
- step_bias: float32 [128], P('tensor'), may hold values from -3 to 0
- log_rate: float32 [128], P('tensor'), may hold values from -4 to 0.7
- skip_gain: float32 [128], P('tensor'), may hold values from 0.5 to 2
- norm_gain: float32 [8192], P('tensor'), may hold values from 0.1 to 1.9
- output_weight: bfloat16 [8192, 8192], P('tensor', 'replica'), may hold values from -0.0625 to 0.0625
- scan_state: float32 [64, 128, 64, 128], P('replica', 'tensor'), may hold values from -6 to 6
- window_x: float32 [64, 3, 8192], P('replica', None, 'tensor'), may hold values from -6 to 6
- window_coeff: float32 [64, 3, 2, 512], P('replica'), may hold values from -6 to 6
Outputs:
- mixed_out: bfloat16 [3, 64, 8192], P(None, 'tensor', 'replica')
- final_state: float32 [64, 128, 64, 128], P('replica', 'tensor')
- final_window_x: float32 [64, 3, 8192], P('replica', None, 'tensor')
- final_window_coeff: float32 [64, 3, 2, 512], P('replica')
The draws below stay inside these ranges and needn't reach their ends.
Inputs may be any that keep to these rules, and one draw needn't show every extreme that they name: On each step, of the 8 rows of one replica (rows of one aligned block of 8), exactly one has its parent on that same replica; two share one parent on another replica; each of the other 5 has its parent on yet another replica, all these replicas distinct. So no other replica holds the parents of more than 2 rows of one replica, nor more than one distinct parent of them. Rows within a block come in any order.
All inputs are finite; a program needn't handle non-finite values.
Results may differ from the reference program's by a relative error of at most 0.005.
Values may be sent and summed in bfloat16 or wider, within the bound.
A program may use at most 192 MiB of HBM per device.

```python
import jax
import jax.numpy as jnp
from jax import lax

D = 8192
P_SIZE = 64
N = 128
K = 4
H = 128
G = 4
ROWS_DEV = 8
STEPS = 3
INNER = 8192
GS = 2048
ROWS = 64


def draw_parents(key, part):
    replicas = ROWS // ROWS_DEV

    def one_block(block_key, dest_replica):
        first_key, second_key, third_key = jax.random.split(block_key, 3)
        offsets = jax.random.permutation(first_key, replicas - 1)[:ROWS_DEV - 2].astype(jnp.int32) + 1
        local_pick = jax.random.randint(second_key, (ROWS_DEV - 1,), 0, ROWS_DEV).astype(jnp.int32)
        source_offset = jnp.concatenate([offsets[:1], offsets, jnp.zeros((1,), jnp.int32)])
        local_row = jnp.concatenate([local_pick[:1], local_pick])
        source = (dest_replica + source_offset) % replicas
        parent_row = source * ROWS_DEV + local_row
        order = jax.random.permutation(third_key, ROWS_DEV)
        return parent_row[order]
    block_keys = jax.random.split(jax.random.fold_in(key, 17), STEPS * replicas)
    dest_list = jnp.tile(jnp.arange(replicas, dtype=jnp.int32), STEPS)
    blocks = jax.vmap(one_block)(block_keys, dest_list)
    return blocks.reshape(STEPS, ROWS).astype(jnp.int32)


def levels(stream_key, extent, shards, least, high):
    gain, own = 1.0, jax.random.fold_in(stream_key, 6)
    for dim, parts in shards:
        heights = jnp.exp(jax.random.uniform(jax.random.fold_in(own, dim), (parts,), jnp.float32, least / len(shards), high / len(shards)))
        gain = gain * jnp.repeat(heights, extent[dim] // parts).reshape([-1 if axis == dim else 1 for axis in range(len(extent))])
    return gain


def bell_draw(stream_key, shape, scale, most, shards=(), held_as=jnp.bfloat16):
    array = scale * jax.random.normal(stream_key, shape, jnp.float32)
    if shards:
        array = array * levels(stream_key, shape, shards, -0.22, 0.18)
    return jnp.clip(array, -most, most).astype(held_as)


def setup_inputs(seed: int = 0) -> dict:
    streams_of = jax.random.split(jax.random.key(seed), 18)
    hidden = bell_draw(streams_of[0], (STEPS, ROWS, D), 1.0, 6.0, ((2, 8),))
    parents = draw_parents(jax.random.fold_in(streams_of[17], 71), 0)
    input_weight = bell_draw(streams_of[2], (D, 2, INNER), D ** -0.5, 0.0625, ((0, 8), (2, 4)))
    coeff_weight = bell_draw(streams_of[3], (D, 2, G * N), D ** -0.5, 0.0625, ((0, 8),))
    step_weight = bell_draw(streams_of[4], (D, H), D ** -0.5, 0.0625, ((0, 8), (1, 4)))
    kernel_x = jnp.clip(jax.random.uniform(streams_of[5], (K, INNER), jnp.float32, -0.5, 0.5) * levels(streams_of[5], (K, INNER), ((1, 4),), -0.4, 0.0), -0.5, 0.5)
    kernel_bias_x = jnp.clip(jax.random.uniform(streams_of[6], (INNER,), jnp.float32, -0.5, 0.5) * levels(streams_of[6], (INNER,), ((0, 4),), -0.4, 0.0), -0.5, 0.5)
    kernel_coeff = jnp.clip(jax.random.uniform(streams_of[7], (K, 2, G * N), jnp.float32, -0.5, 0.5), -0.5, 0.5)
    kernel_bias_coeff = jnp.clip(jax.random.uniform(streams_of[8], (2, G * N), jnp.float32, -0.5, 0.5), -0.5, 0.5)
    step_bias = jnp.clip(-3.0 + 3.0 * jax.random.uniform(streams_of[9], (H,), jnp.float32) ** levels(streams_of[9], (H,), ((0, 4),), -0.2, 0.2), -3.0, 0.0)
    log_rate = jnp.clip(-4.0 + 4.7 * jax.random.uniform(streams_of[10], (H,), jnp.float32) ** levels(streams_of[10], (H,), ((0, 4),), -0.2, 0.2), -4.0, 0.7)
    skip_gain = jnp.clip(0.5 + 1.5 * jax.random.uniform(streams_of[11], (H,), jnp.float32) ** levels(streams_of[11], (H,), ((0, 4),), -0.2, 0.2), 0.5, 2.0)
    norm_gain = jnp.clip(1.0 + 0.18 * jax.random.normal(streams_of[12], (INNER,), jnp.float32), 0.1, 1.9)
    output_weight = bell_draw(streams_of[13], (INNER, D), INNER ** -0.5, 0.0625, ((0, 4), (1, 8)))
    scan_state = bell_draw(streams_of[14], (ROWS, H, P_SIZE, N), 1.0, 6.0, ((0, 8), (1, 4)), jnp.float32)
    window_x = bell_draw(streams_of[15], (ROWS, K - 1, INNER), 1.0, 6.0, ((0, 8), (2, 4)), jnp.float32)
    window_coeff = bell_draw(streams_of[16], (ROWS, K - 1, 2, G * N), 1.0, 6.0, ((0, 8),), jnp.float32)
    return {"hidden": hidden, "parents": parents, "input_weight": input_weight, "coeff_weight": coeff_weight, "step_weight": step_weight, "kernel_x": kernel_x, "kernel_bias_x": kernel_bias_x, "kernel_coeff": kernel_coeff, "kernel_bias_coeff": kernel_bias_coeff, "step_bias": step_bias, "log_rate": log_rate, "skip_gain": skip_gain, "norm_gain": norm_gain, "output_weight": output_weight, "scan_state": scan_state, "window_x": window_x, "window_coeff": window_coeff}


def reference(hidden, parents, input_weight, coeff_weight, step_weight, kernel_x, kernel_bias_x, kernel_coeff, kernel_bias_coeff, step_bias, log_rate, skip_gain, norm_gain, output_weight, scan_state, window_x, window_coeff):
    state = scan_state
    win_x = window_x
    win_coeff = window_coeff
    rate = jnp.exp(log_rate)
    results = []
    for step_index in range(STEPS):
        picks = parents[step_index].astype(jnp.int32)
        state = jnp.take(state, picks, axis=0)
        win_x = jnp.take(win_x, picks, axis=0)
        win_coeff = jnp.take(win_coeff, picks, axis=0)
        step_input = hidden[step_index]
        gate_x = jnp.dot(step_input, input_weight.reshape(D, 2 * INNER), preferred_element_type=jnp.float32).reshape(ROWS, 2, INNER)
        coeffs = jnp.dot(step_input, coeff_weight.reshape(D, 2 * G * N), preferred_element_type=jnp.float32).reshape(ROWS, 2, G * N)
        step_raw = jnp.dot(step_input, step_weight, preferred_element_type=jnp.float32)
        full_x = jnp.concatenate([win_x, gate_x[:, 1][:, None]], axis=1)
        mixed_x = jax.nn.silu(lax.optimization_barrier(jnp.sum(full_x * kernel_x[None], axis=1)) + kernel_bias_x)
        win_x = full_x[:, 1:]
        full_coeff = jnp.concatenate([win_coeff, coeffs[:, None]], axis=1)
        mixed_coeff = jax.nn.silu(lax.optimization_barrier(jnp.sum(full_coeff * kernel_coeff[None], axis=1)) + kernel_bias_coeff)
        win_coeff = full_coeff[:, 1:]
        step_size = jax.nn.softplus(step_raw + step_bias)
        decay = jnp.exp(-rate * step_size)
        heads_x = mixed_x.reshape(ROWS, H, P_SIZE)
        input_b = jnp.repeat(mixed_coeff[:, 0].reshape(ROWS, G, N), H // G, axis=1)
        output_c = jnp.repeat(mixed_coeff[:, 1].reshape(ROWS, G, N), H // G, axis=1)
        state = decay[:, :, None, None] * state + (step_size[:, :, None] * heads_x)[..., None] * input_b[:, :, None, :]
        heads_y = lax.optimization_barrier(jnp.sum(state * output_c[:, :, None, :], axis=-1)) + skip_gain[None, :, None] * heads_x
        flat_y = heads_y.reshape(ROWS, INNER) * jax.nn.silu(gate_x[:, 0])
        grouped = flat_y.reshape(ROWS, H // G, G, P_SIZE)
        scale = lax.rsqrt(lax.optimization_barrier(jnp.sum(grouped * grouped, axis=(1, 3))) / GS + 1e-05)
        normed = ((grouped * scale[:, None, :, None]).reshape(ROWS, INNER) * norm_gain).astype(jnp.bfloat16)
        results.append(jnp.dot(normed, output_weight, preferred_element_type=jnp.float32).astype(jnp.bfloat16))
    return (jnp.stack(results), state, win_x, win_coeff)
```

```python
import jax
import jax.numpy as jnp
from jax import lax
from jax.sharding import PartitionSpec as P

BF = jnp.bfloat16
F32 = jnp.float32


def halves(v):
    high = v.astype(BF)
    return high, (v - high.astype(F32)).astype(BF)


def pick(index, count):
    return (index[:, None] == jnp.arange(count, dtype=jnp.int32)[None, :]).astype(BF)


def dot(a, b):
    return jnp.dot(a, b, preferred_element_type=F32)


def hop(state, parent_row, rows_dev, replicas, me):
    grid = parent_row.reshape(replicas, rows_dev)
    source = grid // rows_dev
    local_row = grid % rows_dev
    matched = source == me
    sending = jnp.max(jnp.where(matched, local_row, 0), axis=1)
    own_source = lax.dynamic_index_in_dim(source, me, 0, keepdims=False)
    own_local = lax.dynamic_index_in_dim(local_row, me, 0, keepdims=False)
    sent = jnp.take(state, sending, axis=0)
    came = lax.all_to_all(sent, "replica", split_axis=0, concat_axis=0, tiled=True)
    rows = []
    for i in range(rows_dev):
        far = lax.dynamic_index_in_dim(came, own_source[i], 0, keepdims=True)
        near = lax.dynamic_index_in_dim(state, own_local[i], 0, keepdims=True)
        rows.append(jnp.where(own_source[i] == me, near, far))
    return jnp.concatenate(rows, axis=0)


def local(
    hidden,
    parents,
    input_weight,
    coeff_weight,
    step_weight,
    kernel_x,
    kernel_bias_x,
    kernel_coeff,
    kernel_bias_coeff,
    step_bias,
    log_rate,
    skip_gain,
    norm_gain,
    output_weight,
    scan_state,
    window_x,
    window_coeff,
):
    rows_dev, heads, head_dim, n = scan_state.shape
    steps, rows, depth = hidden.shape
    taps = kernel_x.shape[0]
    past = taps - 1
    chans = heads * head_dim
    replicas = lax.axis_size("replica")
    tensors = lax.axis_size("tensor")
    me = lax.axis_index("replica")
    mt = lax.axis_index("tensor")
    heads_all = heads * tensors
    groups = kernel_bias_coeff.shape[1] // n
    group_size = heads_all * head_dim // groups
    my_group = mt * heads * groups // heads_all
    coeff_at = my_group * n

    def own_group(v):
        return lax.dynamic_slice_in_dim(v, coeff_at, n, axis=v.ndim - 1)

    moved = scan_state.astype(BF).reshape(rows_dev, heads, head_dim, n)
    start_state = moved
    for s in range(steps):
        moved = hop(moved, parents[s], rows_dev, replicas, me)

    all_rows = jnp.arange(rows, dtype=jnp.int32)
    anc = []
    for s in range(steps):
        path = [all_rows]
        for t in range(s, -1, -1):
            path.append(jnp.take(parents[t], path[-1]))
        anc.append(path[::-1])

    def table_row(s, tau):
        if tau < past:
            return anc[s][0] * past + tau
        t = tau - past
        r = anc[s][t + 1]
        return rows * past + (r // rows_dev) * (steps * rows_dev) + t * rows_dev + r % rows_dev

    def mine(v):
        return lax.dynamic_slice_in_dim(v, me * rows_dev, rows_dev, axis=0)

    wc = own_group(window_coeff).reshape(rows_dev, past, 2 * n)
    wc_hi, wc_lo = halves(wc)
    win = jnp.concatenate([window_x.astype(BF), wc_hi, wc_lo], axis=-1)
    win = win.reshape(rows_dev * past, chans + 4 * n)
    win_all = lax.all_gather(win, "replica", axis=0, tiled=True)

    h = hidden.reshape(steps, replicas, rows_dev, depth).transpose(1, 0, 2, 3)
    h = h.reshape(steps * rows, depth)
    small_w = jnp.concatenate(
        [own_group(coeff_weight).reshape(depth, 2 * n), step_weight], axis=1
    )
    proj = dot(h, input_weight.reshape(depth, 2 * chans))
    small_w = jnp.pad(small_w, ((0, 0), (0, -small_w.shape[1] % 512)))
    small = dot(h, small_w)
    proj = lax.psum_scatter(proj, "replica", scatter_dimension=0, tiled=True)
    small = lax.psum_scatter(small, "replica", scatter_dimension=0, tiled=True)
    gate = proj[:, :chans]
    co_hi, co_lo = halves(small[:, : 2 * n])
    raw_hi, raw_lo = halves(small[:, 2 * n : 2 * n + heads])
    new = jnp.concatenate(
        [proj[:, chans : 2 * chans].astype(BF), co_hi, co_lo, raw_hi, raw_lo], axis=1
    )
    new_all = lax.all_gather(new, "replica", axis=0, tiled=True)
    wide = chans + 4 * n
    table = jnp.concatenate([win_all, new_all[:, :wide]], axis=0)
    raws = new_all[:, wide:]
    entries = table.shape[0]
    table_c = table[:, chans:]

    kern_c = own_group(kernel_coeff).reshape(taps, 2 * n)
    bias_c = own_group(kernel_bias_coeff).reshape(2 * n)

    out_c = []
    for s in range(steps):
        index = jnp.concatenate([table_row(s, s + j) for j in range(taps)])
        got = dot(pick(index, entries), table_c)
        got = (got[:, : 2 * n] + got[:, 2 * n :]).reshape(taps, rows, 2 * n)
        total = jnp.sum(got * kern_c[:, None, :], axis=0) + bias_c
        out_c.append(jax.nn.silu(total[:, n:]).reshape(replicas, 1, rows_dev, n))
    out_c = jnp.concatenate(out_c, axis=1).reshape(replicas * steps * rows_dev, n)
    home = jnp.stack([anc[s][0].reshape(replicas, rows_dev) for s in range(steps)], axis=1)
    home = home.reshape(-1)
    c_hi, c_lo = halves(out_c)
    base = jnp.zeros((2 * steps * rows, chans), F32)
    flat_state = start_state.reshape(rows_dev, chans, n)
    for q in range(rows_dev):
        here = (home == me * rows_dev + q)[:, None]
        lhs = jnp.concatenate(
            [jnp.where(here, c_hi, jnp.zeros_like(c_hi)), jnp.where(here, c_lo, jnp.zeros_like(c_lo))],
            axis=0,
        )
        base = base + lax.dot_general(
            lhs, flat_state[q], (((1,), (1,)), ((), ())), preferred_element_type=F32
        )
    base = (base[: steps * rows] + base[steps * rows :]).astype(BF)
    base = lax.psum_scatter(base, "replica", scatter_dimension=0, tiled=True).astype(F32)

    places = [(s, tau) for s in range(steps) for tau in range(s + taps)]
    index = jnp.concatenate([mine(table_row(s, tau)) for s, tau in places])
    got = dot(pick(index, entries), table)
    got_x = got[:, :chans].reshape(len(places), rows_dev, chans)
    got_c = got[:, chans : chans + 2 * n] + got[:, chans + 2 * n :]
    got_c = got_c.reshape(len(places), rows_dev, 2 * n)
    line_x = {p: got_x[k] for k, p in enumerate(places)}
    line_c = {p: got_c[k] for k, p in enumerate(places)}
    pairs = [(s, t) for s in range(steps) for t in range(s + 1)]
    index = jnp.concatenate([mine(table_row(s, t + past)) - rows * past for s, t in pairs])
    got = dot(pick(index, steps * rows), raws)
    got_raw = (got[:, :heads] + got[:, heads:]).reshape(len(pairs), rows_dev, heads)
    size = {p: jax.nn.softplus(got_raw[k] + step_bias) for k, p in enumerate(pairs)}
    rate = jnp.exp(log_rate)

    def conv(line, kern, bias, s, t):
        total = line[(s, t)] * kern[0]
        for j in range(1, taps):
            total = total + line[(s, t + j)] * kern[j]
        return jax.nn.silu(total + bias)

    norm_group = (mt * heads + jnp.arange(heads, dtype=jnp.int32)) % groups
    member = (norm_group[:, None] == jnp.arange(groups, dtype=jnp.int32)[None, :]).astype(F32)
    heads_y = []
    squares = []
    for s in range(steps):
        xs = [
            conv(line_x, kernel_x, kernel_bias_x, s, t).reshape(rows_dev, heads, head_dim)
            for t in range(s + 1)
        ]
        cs = [conv(line_c, kern_c, bias_c, s, t) for t in range(s + 1)]
        c_now = cs[s][:, n:]
        fade = jnp.ones((rows_dev, heads), F32)
        weights = [None] * (s + 1)
        for t in range(s, -1, -1):
            weights[t] = fade * size[(s, t)]
            fade = fade * jnp.exp(-rate * size[(s, t)])
        own = base[s * rows_dev : (s + 1) * rows_dev].reshape(rows_dev, heads, head_dim)
        y = fade[:, :, None] * own + skip_gain[None, :, None] * xs[s]
        for t in range(s + 1):
            match = jnp.sum(cs[t][:, :n] * c_now, axis=-1, keepdims=True)
            y = y + (weights[t] * match)[:, :, None] * xs[t]
        g = gate[s * rows_dev : (s + 1) * rows_dev].reshape(rows_dev, heads, head_dim)
        y = y * jax.nn.silu(g)
        heads_y.append(y)
        squares.append(
            jnp.dot(jnp.sum(y * y, axis=-1), member, precision=lax.Precision.HIGHEST)
        )
        if s == steps - 1:
            final = fade[:, :, None, None] * moved.astype(F32)
            for t in range(s + 1):
                final = final + (weights[t][:, :, None] * xs[t])[..., None] * (
                    cs[t][:, None, None, :n]
                )
    squares = lax.psum(jnp.concatenate(squares, axis=0), "tensor")
    inverse = lax.rsqrt(squares / group_size + 1e-05)
    head_scale = jnp.dot(inverse, member.T, precision=lax.Precision.HIGHEST)
    gains = norm_gain.reshape(heads, head_dim)
    y = jnp.concatenate(heads_y, axis=0)
    normed = (y * head_scale[:, :, None] * gains[None]).reshape(steps * rows_dev, chans)
    normed = lax.all_gather(normed.astype(BF), "replica", axis=0, tiled=True)
    mixed = lax.psum_scatter(dot(normed, output_weight), "tensor", scatter_dimension=0, tiled=True)
    width = mixed.shape[1]
    mixed = mixed.astype(BF).reshape(-1, steps, rows_dev, width).transpose(1, 0, 2, 3)
    mixed = mixed.reshape(steps, -1, width)

    last = steps - 1
    ends = [last + 1 + j for j in range(past)]
    final_x = jnp.stack([line_x[(last, tau)] for tau in ends], axis=1)
    final_c = jnp.stack([line_c[(last, tau)] for tau in ends], axis=1)
    final_c = lax.all_gather(final_c, "tensor", axis=0)
    final_c = final_c.reshape(groups, tensors // groups, rows_dev, past, 2, n)[:, 0]
    final_c = final_c.transpose(1, 2, 3, 0, 4).reshape(rows_dev, past, 2, groups * n)
    return (mixed, final, final_x, final_c)


def solution(mesh):
    placed = (
        P(None, None, "replica"),
        P(),
        P("replica", None, "tensor"),
        P("replica", None, None),
        P("replica", "tensor"),
        P(None, "tensor"),
        P("tensor"),
        P(),
        P(),
        P("tensor"),
        P("tensor"),
        P("tensor"),
        P("tensor"),
        P("tensor", "replica"),
        P("replica", "tensor", None, None),
        P("replica", None, "tensor"),
        P("replica", None, None, None),
    )
    return jax.shard_map(
        local,
        mesh=mesh,
        in_specs=placed,
        out_specs=(
            P(None, "tensor", "replica"),
            P("replica", "tensor", None, None),
            P("replica", None, "tensor"),
            P("replica", None, None, None),
        ),
        check_vma=False,
    )
```

```python
import jax
import jax.numpy as jnp
from jax import lax
from jax.experimental import pallas as pl
from jax.experimental.pallas import tpu as pltpu
from jax.sharding import PartitionSpec as P

BF = jnp.bfloat16
F32 = jnp.float32


def halves(v):
    high = v.astype(BF)
    return high, (v - high.astype(F32)).astype(BF)


def pick(index, count):
    return (index[:, None] == jnp.arange(count, dtype=jnp.int32)[None, :]).astype(BF)


def dot(a, b):
    return jnp.dot(a, b, preferred_element_type=F32)


def hop(state, parent_row, rows_dev, replicas, me):
    grid = parent_row.reshape(replicas, rows_dev)
    source = grid // rows_dev
    local_row = grid % rows_dev
    matched = source == me
    sending = jnp.max(jnp.where(matched, local_row, 0), axis=1)
    own_source = lax.dynamic_index_in_dim(source, me, 0, keepdims=False)
    own_local = lax.dynamic_index_in_dim(local_row, me, 0, keepdims=False)
    sent = jnp.take(state, sending, axis=0)
    came = lax.all_to_all(sent, "replica", split_axis=0, concat_axis=0, tiled=True)
    rows = []
    for i in range(rows_dev):
        far = lax.dynamic_index_in_dim(came, own_source[i], 0, keepdims=True)
        near = lax.dynamic_index_in_dim(state, own_local[i], 0, keepdims=True)
        rows.append(jnp.where(own_source[i] == me, near, far))
    return jnp.concatenate(rows, axis=0)


def collect(parts, part, row):
    count = part.shape[0]

    def kernel(part_ref, row_ref, *refs):
        sources, out, sems = refs[: len(parts)], refs[len(parts)], refs[len(parts) + 1]
        for i in range(count):
            for p, source in enumerate(sources):

                @pl.when(part_ref[i] == p)
                def _(source=source, i=i):
                    pltpu.make_async_copy(source.at[row_ref[i]], out.at[i], sems.at[i]).start()

        for i in range(count):
            pltpu.make_async_copy(sources[0].at[0], out.at[i], sems.at[i]).wait()

    shape = (count,) + parts[0].shape[1:]
    return pl.pallas_call(
        kernel,
        out_shape=jax.ShapeDtypeStruct(shape, parts[0].dtype),
        in_specs=[pl.BlockSpec(memory_space=pltpu.SMEM)] * 2
        + [pl.BlockSpec(memory_space=pl.ANY)] * len(parts),
        out_specs=pl.BlockSpec(memory_space=pltpu.VMEM),
        scratch_shapes=[pltpu.SemaphoreType.DMA((count,))],
        name="collect",
    )(part, row, *parts)


def capacity(rows_dev, distance):
    return rows_dev // 2 if distance <= 2 else (3 * rows_dev) // 8


def carry(state, first, replicas, me):
    rows_dev = state.shape[0]
    chips = replicas // 2
    chip, core = me // 2, me % 2
    chip_rows = 2 * rows_dev
    rows = jnp.arange(first.shape[0], dtype=jnp.int32)
    swap = [(q, q + 1 - 2 * (q % 2)) for q in range(replicas)]
    beside = lax.ppermute(state, "replica", swap)
    gap = rows // chip_rows - first // chip_rows
    hit = first[None, :] == rows[:, None]
    caps = [capacity(rows_dev, d) for d in range(1, chips)]
    over = jnp.zeros((), jnp.bool_)
    parts = [state, beside]
    ranks = []
    slot = jnp.arange(chip_rows, dtype=jnp.int32)
    for sign in (1, -1):
        far = jnp.max(jnp.where(hit, sign * gap[None, :], 0), axis=1).reshape(chips, chip_rows)
        key = far * chip_rows - slot[None, :]
        rank = jnp.sum((key[:, None, :] > key[:, :, None]).astype(jnp.int32), axis=2)
        for d in range(1, chips):
            counts = jnp.sum((far >= d).astype(jnp.int32), axis=1)
            over = over | (jnp.max(counts) > 2 * caps[d - 1])
        my_rank = lax.dynamic_index_in_dim(rank, chip, 0, keepdims=False)
        places = 2 * jnp.arange(caps[0], dtype=jnp.int32) + core
        order = jnp.sum(jnp.where(my_rank[:, None] == places[None, :], slot[:, None], 0), axis=0)
        side = (order // rows_dev != core).astype(jnp.int32)
        held = collect([state, beside], side, order % rows_dev)
        for d in range(1, chips):
            held = held[: caps[d - 1]]
            pairs = []
            for z in range(chips):
                to = z + sign
                if 0 <= z - sign * (d - 1) < chips and 0 <= to < chips:
                    pairs += [(2 * z + c, 2 * to + c) for c in range(2)]
            held = lax.ppermute(held, "replica", pairs)
            parts.append(held)
        ranks.append(rank.reshape(-1))
    limits = jnp.array([rows_dev] + caps, jnp.int32)

    def seek(owner):
        want = lax.dynamic_slice_in_dim(first, owner * rows_dev, rows_dev, axis=0)
        step = chip - want // chip_rows
        dist = jnp.abs(step)
        rank = jnp.where(step > 0, ranks[0][want], ranks[1][want])
        part = jnp.where(step > 0, 1 + dist, chips + dist)
        aside = ((want // rows_dev) % 2 != core).astype(jnp.int32)
        part = jnp.where(step == 0, aside, part)
        row = jnp.where(step == 0, want % rows_dev, jnp.minimum(rank // 2, limits[dist] - 1))
        return part, row, (step == 0) | (rank % 2 == core)

    part, row, _ = seek(chip * 2 + 1 - core)
    came = lax.ppermute(collect(parts, part, row), "replica", swap)
    part, row, near = seek(me)
    return jnp.where(near[:, None, None, None], collect(parts, part, row), came), over


def local(
    hidden,
    parents,
    input_weight,
    coeff_weight,
    step_weight,
    kernel_x,
    kernel_bias_x,
    kernel_coeff,
    kernel_bias_coeff,
    step_bias,
    log_rate,
    skip_gain,
    norm_gain,
    output_weight,
    scan_state,
    window_x,
    window_coeff,
):
    rows_dev, heads, head_dim, n = scan_state.shape
    steps, rows, depth = hidden.shape
    taps = kernel_x.shape[0]
    past = taps - 1
    chans = heads * head_dim
    replicas = lax.axis_size("replica")
    tensors = lax.axis_size("tensor")
    me = lax.axis_index("replica")
    mt = lax.axis_index("tensor")
    heads_all = heads * tensors
    groups = kernel_bias_coeff.shape[1] // n
    group_size = heads_all * head_dim // groups
    my_group = mt * heads * groups // heads_all
    coeff_at = my_group * n

    def own_group(v):
        return lax.dynamic_slice_in_dim(v, coeff_at, n, axis=v.ndim - 1)

    all_rows = jnp.arange(rows, dtype=jnp.int32)
    anc = []
    for s in range(steps):
        path = [all_rows]
        for t in range(s, -1, -1):
            path.append(jnp.take(parents[t], path[-1]))
        anc.append(path[::-1])

    def table_row(s, tau):
        if tau < past:
            return anc[s][0] * past + tau
        t = tau - past
        r = anc[s][t + 1]
        return rows * past + (r // rows_dev) * (steps * rows_dev) + t * rows_dev + r % rows_dev

    def mine(v):
        return lax.dynamic_slice_in_dim(v, me * rows_dev, rows_dev, axis=0)

    moved, over = carry(scan_state.astype(BF), anc[-1][0], replicas, me)

    wc = own_group(window_coeff).reshape(rows_dev, past, 2 * n)
    wc_hi, wc_lo = halves(wc)
    win = jnp.concatenate([window_x.astype(BF), wc_hi, wc_lo], axis=-1)
    win = win.reshape(rows_dev * past, chans + 4 * n)
    win_all = lax.all_gather(win, "replica", axis=0, tiled=True)

    h = hidden.reshape(steps, replicas, rows_dev, depth).transpose(1, 0, 2, 3)
    h = h.reshape(steps * rows, depth)
    small_w = jnp.concatenate(
        [own_group(coeff_weight).reshape(depth, 2 * n), step_weight], axis=1
    )
    proj = jnp.einsum("rd,dkc->rkc", h, input_weight, preferred_element_type=F32)
    small_w = jnp.pad(small_w, ((0, 0), (0, -small_w.shape[1] % 512)))
    small = dot(h, small_w)
    proj = lax.psum_scatter(proj, "replica", scatter_dimension=0, tiled=True)
    small = lax.psum_scatter(small, "replica", scatter_dimension=0, tiled=True)
    gate = proj[:, 0]
    co_hi, co_lo = halves(small[:, : 2 * n])
    raw_hi, raw_lo = halves(small[:, 2 * n : 2 * n + heads])
    new = jnp.concatenate(
        [proj[:, 1].astype(BF), co_hi, co_lo, raw_hi, raw_lo], axis=1
    )
    new_all = lax.all_gather(new, "replica", axis=0, tiled=True)
    wide = chans + 4 * n
    table = jnp.concatenate([win_all, new_all[:, :wide]], axis=0)
    raws = new_all[:, wide:]
    entries = table.shape[0]
    table_c = table[:, chans:]

    kern_c = own_group(kernel_coeff).reshape(taps, 2 * n)
    bias_c = own_group(kernel_bias_coeff).reshape(2 * n)

    out_c = []
    for s in range(steps):
        index = jnp.concatenate([table_row(s, s + j) for j in range(taps)])
        got = dot(pick(index, entries), table_c)
        got = (got[:, : 2 * n] + got[:, 2 * n :]).reshape(taps, rows, 2 * n)
        total = jnp.sum(got * kern_c[:, None, :], axis=0) + bias_c
        out_c.append(jax.nn.silu(total[:, n:]).reshape(replicas, 1, rows_dev, n))
    out_c = jnp.concatenate(out_c, axis=1).reshape(replicas * steps * rows_dev, n)
    home = jnp.stack([anc[s][0].reshape(replicas, rows_dev) for s in range(steps)], axis=1)
    home = home.reshape(-1)
    c_hi, c_lo = halves(out_c)
    base = jnp.zeros((2 * steps * rows, chans), F32)
    s_hi, s_lo = halves(scan_state.reshape(rows_dev, chans, n))
    for q in range(rows_dev):
        here = (home == me * rows_dev + q)[:, None]
        lhs = jnp.concatenate(
            [jnp.where(here, c_hi, jnp.zeros_like(c_hi)), jnp.where(here, c_lo, jnp.zeros_like(c_lo))],
            axis=0,
        )
        for part in (s_hi, s_lo):
            base = base + lax.dot_general(
                lhs, part[q], (((1,), (1,)), ((), ())), preferred_element_type=F32
            )
    base = base[: steps * rows] + base[steps * rows :]
    base = lax.psum_scatter(base, "replica", scatter_dimension=0, tiled=True)

    places = [(s, tau) for s in range(steps) for tau in range(s + taps)]
    index = jnp.concatenate([mine(table_row(s, tau)) for s, tau in places])
    got = dot(pick(index, entries), table)
    got_x = got[:, :chans].reshape(len(places), rows_dev, chans)
    got_c = got[:, chans : chans + 2 * n] + got[:, chans + 2 * n :]
    got_c = got_c.reshape(len(places), rows_dev, 2 * n)
    line_x = {p: got_x[k] for k, p in enumerate(places)}
    line_c = {p: got_c[k] for k, p in enumerate(places)}
    pairs = [(s, t) for s in range(steps) for t in range(s + 1)]
    index = jnp.concatenate([mine(table_row(s, t + past)) - rows * past for s, t in pairs])
    got = dot(pick(index, steps * rows), raws)
    got_raw = (got[:, :heads] + got[:, heads:]).reshape(len(pairs), rows_dev, heads)
    size = {p: jax.nn.softplus(got_raw[k] + step_bias) for k, p in enumerate(pairs)}
    rate = jnp.exp(log_rate)

    def conv(line, kern, bias, s, t):
        total = line[(s, t)] * kern[0]
        for j in range(1, taps):
            total = total + line[(s, t + j)] * kern[j]
        return jax.nn.silu(total + bias)

    norm_group = (mt * heads + jnp.arange(heads, dtype=jnp.int32)) % groups
    member = (norm_group[:, None] == jnp.arange(groups, dtype=jnp.int32)[None, :]).astype(F32)

    def hops():
        state = scan_state.astype(BF)
        for s in range(steps):
            state = hop(state, parents[s], rows_dev, replicas, me)
        return state

    first_moved = moved
    heads_y = []
    squares = []
    for s in range(steps):
        xs = [
            conv(line_x, kernel_x, kernel_bias_x, s, t).reshape(rows_dev, heads, head_dim)
            for t in range(s + 1)
        ]
        cs = [conv(line_c, kern_c, bias_c, s, t) for t in range(s + 1)]
        c_now = cs[s][:, n:]
        fade = jnp.ones((rows_dev, heads), F32)
        weights = [None] * (s + 1)
        for t in range(s, -1, -1):
            weights[t] = fade * size[(s, t)]
            fade = fade * jnp.exp(-rate * size[(s, t)])
        own = base[s * rows_dev : (s + 1) * rows_dev].reshape(rows_dev, heads, head_dim)
        y = fade[:, :, None] * own + skip_gain[None, :, None] * xs[s]
        for t in range(s + 1):
            match = jnp.sum(cs[t][:, :n] * c_now, axis=-1, keepdims=True)
            y = y + (weights[t] * match)[:, :, None] * xs[t]
        g = gate[s * rows_dev : (s + 1) * rows_dev].reshape(rows_dev, heads, head_dim)
        y = y * jax.nn.silu(g)
        heads_y.append(y)
        squares.append(
            jnp.dot(jnp.sum(y * y, axis=-1), member, precision=lax.Precision.HIGHEST)
        )
        if s == steps - 1:
            moved = lax.cond(over, hops, lambda: first_moved)
            final = fade[:, :, None, None] * moved.astype(F32)
            for t in range(s + 1):
                final = final + (weights[t][:, :, None] * xs[t])[..., None] * (
                    cs[t][:, None, None, :n]
                )
    squares = lax.psum(jnp.concatenate(squares, axis=0), "tensor")
    inverse = lax.rsqrt(squares / group_size + 1e-05)
    head_scale = jnp.dot(inverse, member.T, precision=lax.Precision.HIGHEST)
    gains = norm_gain.reshape(heads, head_dim)
    y = jnp.concatenate(heads_y, axis=0)
    normed = (y * head_scale[:, :, None] * gains[None]).reshape(steps * rows_dev, chans)
    normed = lax.all_gather(normed.astype(BF), "replica", axis=0, tiled=True)
    mixed = lax.psum_scatter(dot(normed, output_weight), "tensor", scatter_dimension=0, tiled=True)
    width = mixed.shape[1]
    mixed = mixed.astype(BF).reshape(-1, steps, rows_dev, width).transpose(1, 0, 2, 3)
    mixed = mixed.reshape(steps, -1, width)

    last = steps - 1
    ends = [last + 1 + j for j in range(past)]
    final_x = jnp.stack([line_x[(last, tau)] for tau in ends], axis=1)
    final_c = jnp.stack([line_c[(last, tau)] for tau in ends], axis=1)
    final_c = lax.all_gather(final_c, "tensor", axis=0)
    final_c = final_c.reshape(groups, tensors // groups, rows_dev, past, 2, n)[:, 0]
    final_c = final_c.transpose(1, 2, 3, 0, 4).reshape(rows_dev, past, 2, groups * n)
    return (mixed, final, final_x, final_c)


def solution(mesh):
    placed = (
        P(None, None, "replica"),
        P(),
        P("replica", None, "tensor"),
        P("replica", None, None),
        P("replica", "tensor"),
        P(None, "tensor"),
        P("tensor"),
        P(),
        P(),
        P("tensor"),
        P("tensor"),
        P("tensor"),
        P("tensor"),
        P("tensor", "replica"),
        P("replica", "tensor", None, None),
        P("replica", None, "tensor"),
        P("replica", None, None, None),
    )
    return jax.shard_map(
        local,
        mesh=mesh,
        in_specs=placed,
        out_specs=(
            P(None, "tensor", "replica"),
            P("replica", "tensor", None, None),
            P("replica", None, "tensor"),
            P("replica", None, None, None),
        ),
        check_vma=False,
    )
```

```python
import jax
import jax.numpy as jnp
from jax import lax
from jax.experimental import pallas as pl
from jax.experimental.pallas import tpu as pltpu
from jax.sharding import PartitionSpec as P

BF = jnp.bfloat16
F32 = jnp.float32


def halves(v):
    high = v.astype(BF)
    return high, (v - high.astype(F32)).astype(BF)


def pick(index, count):
    return (index[:, None] == jnp.arange(count, dtype=jnp.int32)[None, :]).astype(BF)


def dot(a, b):
    return jnp.dot(a, b, preferred_element_type=F32)


def hop(state, parent_row, rows_dev, replicas, me):
    grid = parent_row.reshape(replicas, rows_dev)
    source = grid // rows_dev
    local_row = grid % rows_dev
    matched = source == me
    sending = jnp.max(jnp.where(matched, local_row, 0), axis=1)
    own_source = lax.dynamic_index_in_dim(source, me, 0, keepdims=False)
    own_local = lax.dynamic_index_in_dim(local_row, me, 0, keepdims=False)
    sent = jnp.take(state, sending, axis=0)
    came = lax.all_to_all(sent, "replica", split_axis=0, concat_axis=0, tiled=True)
    rows = []
    for i in range(rows_dev):
        far = lax.dynamic_index_in_dim(came, own_source[i], 0, keepdims=True)
        near = lax.dynamic_index_in_dim(state, own_local[i], 0, keepdims=True)
        rows.append(jnp.where(own_source[i] == me, near, far))
    return jnp.concatenate(rows, axis=0)


def collect(parts, part, row):
    count = part.shape[0]

    def kernel(part_ref, row_ref, *refs):
        sources, out, sems = refs[: len(parts)], refs[len(parts)], refs[len(parts) + 1]
        for i in range(count):
            for p, source in enumerate(sources):

                @pl.when(part_ref[i] == p)
                def _(source=source, i=i):
                    pltpu.make_async_copy(source.at[row_ref[i]], out.at[i], sems.at[i]).start()

        for i in range(count):
            pltpu.make_async_copy(sources[0].at[0], out.at[i], sems.at[i]).wait()

    shape = (count,) + parts[0].shape[1:]
    return pl.pallas_call(
        kernel,
        out_shape=jax.ShapeDtypeStruct(shape, parts[0].dtype),
        in_specs=[pl.BlockSpec(memory_space=pltpu.SMEM)] * 2
        + [pl.BlockSpec(memory_space=pl.ANY)] * len(parts),
        out_specs=pl.BlockSpec(memory_space=pltpu.VMEM),
        scratch_shapes=[pltpu.SemaphoreType.DMA((count,))],
        name="collect",
    )(part, row, *parts)


def capacity(rows_dev, distance):
    return rows_dev // 2 if distance <= 2 else (3 * rows_dev) // 8


def carry(state, first, replicas, me):
    rows_dev = state.shape[0]
    chips = replicas // 2
    chip, core = me // 2, me % 2
    chip_rows = 2 * rows_dev
    rows = jnp.arange(first.shape[0], dtype=jnp.int32)
    swap = [(q, q + 1 - 2 * (q % 2)) for q in range(replicas)]
    beside = lax.ppermute(state, "replica", swap)
    gap = rows // chip_rows - first // chip_rows
    hit = first[None, :] == rows[:, None]
    caps = [capacity(rows_dev, d) for d in range(1, chips)]
    over = jnp.zeros((), jnp.bool_)
    parts = [state, beside]
    ranks = []
    slot = jnp.arange(chip_rows, dtype=jnp.int32)
    for sign in (1, -1):
        far = jnp.max(jnp.where(hit, sign * gap[None, :], 0), axis=1).reshape(chips, chip_rows)
        key = far * chip_rows - slot[None, :]
        rank = jnp.sum((key[:, None, :] > key[:, :, None]).astype(jnp.int32), axis=2)
        for d in range(1, chips):
            counts = jnp.sum((far >= d).astype(jnp.int32), axis=1)
            over = over | (jnp.max(counts) > 2 * caps[d - 1])
        my_rank = lax.dynamic_index_in_dim(rank, chip, 0, keepdims=False)
        places = 2 * jnp.arange(caps[0], dtype=jnp.int32) + core
        order = jnp.sum(jnp.where(my_rank[:, None] == places[None, :], slot[:, None], 0), axis=0)
        side = (order // rows_dev != core).astype(jnp.int32)
        held = collect([state, beside], side, order % rows_dev)
        for d in range(1, chips):
            held = held[: caps[d - 1]]
            pairs = []
            for z in range(chips):
                to = z + sign
                if 0 <= z - sign * (d - 1) < chips and 0 <= to < chips:
                    pairs += [(2 * z + c, 2 * to + c) for c in range(2)]
            held = lax.ppermute(held, "replica", pairs)
            parts.append(held)
        ranks.append(rank.reshape(-1))
    limits = jnp.array([rows_dev] + caps, jnp.int32)

    def seek(owner):
        want = lax.dynamic_slice_in_dim(first, owner * rows_dev, rows_dev, axis=0)
        step = chip - want // chip_rows
        dist = jnp.abs(step)
        rank = jnp.where(step > 0, ranks[0][want], ranks[1][want])
        part = jnp.where(step > 0, 1 + dist, chips + dist)
        aside = ((want // rows_dev) % 2 != core).astype(jnp.int32)
        part = jnp.where(step == 0, aside, part)
        row = jnp.where(step == 0, want % rows_dev, jnp.minimum(rank // 2, limits[dist] - 1))
        return part, row, (step == 0) | (rank % 2 == core)

    part, row, _ = seek(chip * 2 + 1 - core)
    came = lax.ppermute(collect(parts, part, row), "replica", swap)
    part, row, near = seek(me)
    return jnp.where(near[:, None, None, None], collect(parts, part, row), came), over


def local(
    hidden,
    parents,
    input_weight,
    coeff_weight,
    step_weight,
    kernel_x,
    kernel_bias_x,
    kernel_coeff,
    kernel_bias_coeff,
    step_bias,
    log_rate,
    skip_gain,
    norm_gain,
    output_weight,
    scan_state,
    window_x,
    window_coeff,
):
    rows_dev, heads, head_dim, n = scan_state.shape
    steps, rows, depth = hidden.shape
    taps = kernel_x.shape[0]
    past = taps - 1
    chans = heads * head_dim
    replicas = lax.axis_size("replica")
    tensors = lax.axis_size("tensor")
    me = lax.axis_index("replica")
    mt = lax.axis_index("tensor")
    heads_all = heads * tensors
    groups = kernel_bias_coeff.shape[1] // n
    group_size = heads_all * head_dim // groups
    my_group = mt * heads * groups // heads_all
    coeff_at = my_group * n

    def own_group(v):
        return lax.dynamic_slice_in_dim(v, coeff_at, n, axis=v.ndim - 1)

    all_rows = jnp.arange(rows, dtype=jnp.int32)
    anc = []
    for s in range(steps):
        path = [all_rows]
        for t in range(s, -1, -1):
            path.append(jnp.take(parents[t], path[-1]))
        anc.append(path[::-1])

    def table_row(s, tau):
        if tau < past:
            return anc[s][0] * past + tau
        t = tau - past
        r = anc[s][t + 1]
        return rows * past + (r // rows_dev) * (steps * rows_dev) + t * rows_dev + r % rows_dev

    def mine(v):
        return lax.dynamic_slice_in_dim(v, me * rows_dev, rows_dev, axis=0)

    moved, over = carry(scan_state.astype(BF), anc[-1][0], replicas, me)

    wc = own_group(window_coeff).reshape(rows_dev, past, 2 * n)
    wc_hi, wc_lo = halves(wc)
    win = jnp.concatenate([window_x.astype(BF), wc_hi, wc_lo], axis=-1)
    win = win.reshape(rows_dev * past, chans + 4 * n)
    win_all = lax.all_gather(win, "replica", axis=0, tiled=True)

    h = hidden.reshape(steps, replicas, rows_dev, depth).transpose(1, 0, 2, 3)
    h = h.reshape(steps * rows, depth)
    small_w = jnp.concatenate(
        [own_group(coeff_weight).reshape(depth, 2 * n), step_weight], axis=1
    )
    proj = jnp.einsum("rd,dkc->rkc", h, input_weight, preferred_element_type=F32)
    small_w = jnp.pad(small_w, ((0, 0), (0, -small_w.shape[1] % 512)))
    small = dot(h, small_w)
    proj = lax.psum_scatter(proj, "replica", scatter_dimension=0, tiled=True)
    small = lax.psum_scatter(small, "replica", scatter_dimension=0, tiled=True)
    gate = proj[:, 0]
    co_hi, co_lo = halves(small[:, : 2 * n])
    raw_hi, raw_lo = halves(small[:, 2 * n : 2 * n + heads])
    new = jnp.concatenate(
        [proj[:, 1].astype(BF), co_hi, co_lo, raw_hi, raw_lo], axis=1
    )
    new_all = lax.all_gather(new, "replica", axis=0, tiled=True)
    wide = chans + 4 * n
    table = jnp.concatenate([win_all, new_all[:, :wide]], axis=0)
    raws = new_all[:, wide:]
    entries = table.shape[0]
    table_c = table[:, chans:]

    kern_c = own_group(kernel_coeff).reshape(taps, 2 * n)
    bias_c = own_group(kernel_bias_coeff).reshape(2 * n)

    out_c = []
    for s in range(steps):
        index = jnp.concatenate([table_row(s, s + j) for j in range(taps)])
        got = dot(pick(index, entries), table_c)
        got = (got[:, : 2 * n] + got[:, 2 * n :]).reshape(taps, rows, 2 * n)
        total = jnp.sum(got * kern_c[:, None, :], axis=0) + bias_c
        out_c.append(jax.nn.silu(total[:, n:]).reshape(replicas, 1, rows_dev, n))
    out_c = jnp.concatenate(out_c, axis=1).reshape(replicas * steps * rows_dev, n)
    home = jnp.stack([anc[s][0].reshape(replicas, rows_dev) for s in range(steps)], axis=1)
    home = home.reshape(-1)
    c_hi, c_lo = halves(out_c)
    base = jnp.zeros((2 * steps * rows, chans), F32)
    flat_state = scan_state.astype(BF).reshape(rows_dev, chans, n)
    for q in range(rows_dev):
        here = (home == me * rows_dev + q)[:, None]
        lhs = jnp.concatenate(
            [jnp.where(here, c_hi, jnp.zeros_like(c_hi)), jnp.where(here, c_lo, jnp.zeros_like(c_lo))],
            axis=0,
        )
        base = base + lax.dot_general(
            lhs, flat_state[q], (((1,), (1,)), ((), ())), preferred_element_type=F32
        )
    base = base[: steps * rows] + base[steps * rows :]
    base = lax.psum_scatter(base, "replica", scatter_dimension=0, tiled=True)

    places = [(s, tau) for s in range(steps) for tau in range(s + taps)]
    index = jnp.concatenate([mine(table_row(s, tau)) for s, tau in places])
    got = dot(pick(index, entries), table)
    got_x = got[:, :chans].reshape(len(places), rows_dev, chans)
    got_c = got[:, chans : chans + 2 * n] + got[:, chans + 2 * n :]
    got_c = got_c.reshape(len(places), rows_dev, 2 * n)
    line_x = {p: got_x[k] for k, p in enumerate(places)}
    line_c = {p: got_c[k] for k, p in enumerate(places)}
    pairs = [(s, t) for s in range(steps) for t in range(s + 1)]
    index = jnp.concatenate([mine(table_row(s, t + past)) - rows * past for s, t in pairs])
    got = dot(pick(index, steps * rows), raws)
    got_raw = (got[:, :heads] + got[:, heads:]).reshape(len(pairs), rows_dev, heads)
    size = {p: jax.nn.softplus(got_raw[k] + step_bias) for k, p in enumerate(pairs)}
    rate = jnp.exp(log_rate)

    def conv(line, kern, bias, s, t):
        total = line[(s, t)] * kern[0]
        for j in range(1, taps):
            total = total + line[(s, t + j)] * kern[j]
        return jax.nn.silu(total + bias)

    norm_group = (mt * heads + jnp.arange(heads, dtype=jnp.int32)) % groups
    member = (norm_group[:, None] == jnp.arange(groups, dtype=jnp.int32)[None, :]).astype(F32)

    def hops():
        state = scan_state.astype(BF)
        for s in range(steps):
            state = hop(state, parents[s], rows_dev, replicas, me)
        return state

    first_moved = moved
    heads_y = []
    squares = []
    for s in range(steps):
        xs = [
            conv(line_x, kernel_x, kernel_bias_x, s, t).reshape(rows_dev, heads, head_dim)
            for t in range(s + 1)
        ]
        cs = [conv(line_c, kern_c, bias_c, s, t) for t in range(s + 1)]
        c_now = cs[s][:, n:]
        fade = jnp.ones((rows_dev, heads), F32)
        weights = [None] * (s + 1)
        for t in range(s, -1, -1):
            weights[t] = fade * size[(s, t)]
            fade = fade * jnp.exp(-rate * size[(s, t)])
        own = base[s * rows_dev : (s + 1) * rows_dev].reshape(rows_dev, heads, head_dim)
        y = fade[:, :, None] * own + skip_gain[None, :, None] * xs[s]
        for t in range(s + 1):
            match = jnp.sum(cs[t][:, :n] * c_now, axis=-1, keepdims=True)
            y = y + (weights[t] * match)[:, :, None] * xs[t]
        g = gate[s * rows_dev : (s + 1) * rows_dev].reshape(rows_dev, heads, head_dim)
        y = y * jax.nn.silu(g)
        heads_y.append(y)
        squares.append(
            jnp.dot(jnp.sum(y * y, axis=-1), member, precision=lax.Precision.HIGHEST)
        )
        if s == steps - 1:
            moved = lax.cond(over, hops, lambda: first_moved)
            final = fade[:, :, None, None] * moved.astype(F32)
            for t in range(s + 1):
                final = final + (weights[t][:, :, None] * xs[t])[..., None] * (
                    cs[t][:, None, None, :n]
                )
    squares = lax.psum(jnp.concatenate(squares, axis=0), "tensor")
    inverse = lax.rsqrt(squares / group_size + 1e-05)
    head_scale = jnp.dot(inverse, member.T, precision=lax.Precision.HIGHEST)
    gains = norm_gain.reshape(heads, head_dim)
    y = jnp.concatenate(heads_y, axis=0)
    normed = (y * head_scale[:, :, None] * gains[None]).reshape(steps * rows_dev, chans)
    normed = lax.all_gather(normed.astype(BF), "replica", axis=0, tiled=True)
    mixed = lax.psum_scatter(dot(normed, output_weight), "tensor", scatter_dimension=0, tiled=True)
    width = mixed.shape[1]
    mixed = mixed.astype(BF).reshape(-1, steps, rows_dev, width).transpose(1, 0, 2, 3)
    mixed = mixed.reshape(steps, -1, width)

    last = steps - 1
    ends = [last + 1 + j for j in range(past)]
    final_x = jnp.stack([line_x[(last, tau)] for tau in ends], axis=1)
    final_c = jnp.stack([line_c[(last, tau)] for tau in ends], axis=1)
    final_c = lax.all_gather(final_c, "tensor", axis=0)
    final_c = final_c.reshape(groups, tensors // groups, rows_dev, past, 2, n)[:, 0]
    final_c = final_c.transpose(1, 2, 3, 0, 4).reshape(rows_dev, past, 2, groups * n)
    return (mixed, final, final_x, final_c)


def solution(mesh):
    placed = (
        P(None, None, "replica"),
        P(),
        P("replica", None, "tensor"),
        P("replica", None, None),
        P("replica", "tensor"),
        P(None, "tensor"),
        P("tensor"),
        P(),
        P(),
        P("tensor"),
        P("tensor"),
        P("tensor"),
        P("tensor"),
        P("tensor", "replica"),
        P("replica", "tensor", None, None),
        P("replica", None, "tensor"),
        P("replica", None, None, None),
    )
    return jax.shard_map(
        local,
        mesh=mesh,
        in_specs=placed,
        out_specs=(
            P(None, "tensor", "replica"),
            P("replica", "tensor", None, None),
            P("replica", None, "tensor"),
            P("replica", None, None, None),
        ),
        check_vma=False,
    )
```
